32 devices in a mesh: grp: 2 (over y), gene: 4 (over z), cell: 4 (over x, core).
Axes of the slice: x: 2, y: 2, z: 4, core: 2. Of those that a mesh axis runs over, the one named last changes fastest.
Arguments:
- expression: bfloat16 [4096, 32768], P(('grp', 'cell'), 'gene'), parts along dimension 0, may hold values from -6 to 6
- gene_mask: int32 [4096, 32768], P(('grp', 'cell'), 'gene'), parts along dimension 0, may hold values 0 or 1
- mask_value: bfloat16 [32768], P('gene'), may hold values from -4 to 4
- w_qkv: bfloat16 [32768, 3072], P('gene'), may hold values from -0.03125 to 0.03125
- w_out: bfloat16 [1024, 32768], P(None, 'gene'), may hold values from -1.5 to 1.5
- w_first: bfloat16 [128, 256, 256], P('gene'), may hold values from -0.375 to 0.375
- w_second: bfloat16 [128, 256, 256], P('gene'), may hold values from -0.375 to 0.375
- cotangent: bfloat16 [4096, 32768], P(('grp', 'cell'), 'gene'), parts along dimension 0, may hold values from -6 to 6
Outputs:
- denoised: bfloat16 [4096, 32768], P(('grp', 'cell'), 'gene'), parts along dimension 0
- grad_first: float32 [256, 256, 256], P(('grp', 'gene'), 'cell'), parts along dimension 0
- grad_second: float32 [256, 256, 256], P(('grp', 'gene'), 'cell'), parts along dimension 0
The draws below stay inside these ranges and needn't reach their ends.
There are 2 independent parts, one for each index of `grp`. The reference program is written for one: setup_inputs(seed, part) draws one part's arguments, and reference() takes and returns one part's arrays. A program takes and returns all parts, laid end to end along the dimension named above; an argument that names none is the same for every part. Nothing has to cross between parts.
All inputs are finite; a program needn't handle non-finite values. No bound on the sum of `gene_mask` on one device may be relied on, other than what follows from the above.
Results may differ from the reference program's by a relative error of at most 0.02.
Values may be sent and summed in bfloat16 or wider, within the bound.
A program may use at most 256 MiB of HBM per device.

```python
import jax
import jax.numpy as jnp
from jax import lax

NB = 128
BS = 256
HEADS = 16
HEAD_DIM = 64
G = 32768
WIDTH = 1024
CELLS = 2048


def plant(entries, stream_key, least, high):
    longest = entries.shape.index(max(entries.shape))
    spots = []
    for shift in (0, 1):
        where = [jax.random.randint(jax.random.fold_in(stream_key, axis), (), 0, length) for axis, length in enumerate(entries.shape)]
        where[longest] = (where[longest] + shift) % entries.shape[longest]
        spots.append(tuple(where))
    return entries.at[spots[0]].set(least).at[spots[1]].set(high)


def shard_levels(stream_key, dims, shards, smallest, largest):
    def one(dim, parts):
        heights = jax.random.uniform(jax.random.fold_in(jax.random.fold_in(stream_key, 6), dim), (parts,), jnp.float32, smallest / len(shards), largest / len(shards))
        return jnp.repeat(jnp.exp(heights), dims[dim] // parts).reshape((-1,) + (1,) * (len(dims) - dim - 1))

    gain = one(*shards[0])
    for cut in shards[1:]:
        gain = gain * one(*cut)
    return gain


def bell_draw(stream_key, shape, width, reach, split=(), kind=jnp.bfloat16):
    result = width * jax.random.normal(stream_key, shape, jnp.float32)
    if split:
        result = result * shard_levels(stream_key, shape, split, -0.22, 0.18)
    return jnp.clip(result, -reach, reach).astype(kind)


def setup_inputs(seed: int = 0, part: int = 0) -> dict:
    streams_of = jax.random.split(jax.random.key(seed), 9)
    part_keys = jax.random.split(jax.random.fold_in(streams_of[8], part), 9)
    return {
        "expression": bell_draw(part_keys[0], (CELLS, G), 1.0, 6.0, ((0, 4), (1, 4))),
        "gene_mask": plant((jax.random.randint(part_keys[1], (CELLS, G), 0, 4) < 1).astype(jnp.int32), jax.random.fold_in(part_keys[1], 1), 0, 1),
        "mask_value": bell_draw(streams_of[2], (G,), 1.0, 4.0, ((0, 4),)),
        "w_qkv": bell_draw(streams_of[3], (G, 3 * WIDTH), G ** -0.5, 0.03125, ((0, 4),)),
        "w_out": bell_draw(streams_of[4], (WIDTH, G), (WIDTH // 64) ** -0.5, 1.5, ((1, 4),)),
        "w_first": bell_draw(streams_of[5], (NB, BS, BS), BS ** -0.5, 0.375, ((0, 4),)),
        "w_second": bell_draw(streams_of[6], (NB, BS, BS), BS ** -0.5, 0.375, ((0, 4),)),
        "cotangent": bell_draw(part_keys[7], (CELLS, G), 1.0, 6.0, ((0, 4), (1, 4))),
    }


def normalize(part, count):
    shaped = part.reshape(count, HEADS, HEAD_DIM)
    meansq = lax.optimization_barrier(jnp.mean(shaped * shaped, axis=-1, keepdims=True))
    return (shaped * lax.rsqrt(meansq + 1e-06)).astype(jnp.bfloat16)

def reference(expression, gene_mask, mask_value, w_qkv, w_out, w_first, w_second, cotangent):
    count = expression.shape[0]
    masked_in = jnp.where(gene_mask == 1, mask_value[None, :], expression)
    qkv = jnp.dot(masked_in, w_qkv, preferred_element_type=jnp.float32)
    queries = normalize(qkv[:, :WIDTH], count)
    keys_normed = normalize(qkv[:, WIDTH:2 * WIDTH], count)
    values_b = qkv[:, 2 * WIDTH:].reshape(count, HEADS, HEAD_DIM).astype(jnp.bfloat16)
    scores = jnp.einsum('qhd,khd->hqk', queries.astype(jnp.float32), keys_normed.astype(jnp.float32)) * HEAD_DIM ** (-0.5)
    expw = jnp.exp(scores).astype(jnp.bfloat16)
    denom = lax.optimization_barrier(jnp.sum(expw.astype(jnp.float32), axis=2))
    numer = jnp.einsum('hqk,khd->qhd', expw.astype(jnp.float32), values_b.astype(jnp.float32))
    attended = (numer / denom.T[:, :, None]).astype(jnp.bfloat16).reshape(count, WIDTH)
    added = jnp.dot(attended, w_out, preferred_element_type=jnp.float32)
    hidden = (masked_in.astype(jnp.float32) + added).astype(jnp.bfloat16)
    blocks = hidden.reshape(count, NB, BS)
    first = jnp.einsum('cbi,bio->cbo', blocks.astype(jnp.float32), w_first.astype(jnp.float32)).astype(jnp.bfloat16)
    permuted = jnp.swapaxes(first, 1, 2).reshape(count, NB, BS)
    mixed = jnp.einsum('cjk,jko->cjo', permuted.astype(jnp.float32), w_second.astype(jnp.float32))
    denoised = (blocks.astype(jnp.float32) + mixed).astype(jnp.bfloat16).reshape(count, NB * BS)
    cot_blocks = cotangent.reshape(count, NB, BS).astype(jnp.float32)
    grad_second = jnp.einsum('cjk,cjo->jko', permuted.astype(jnp.float32), cot_blocks)
    back_perm = jnp.einsum('cjo,jko->cjk', cot_blocks, w_second.astype(jnp.float32)).astype(jnp.bfloat16)
    back_first = jnp.swapaxes(back_perm.reshape(count, BS, NB), 1, 2)
    grad_first = jnp.einsum('cbi,cbo->bio', blocks.astype(jnp.float32), back_first.astype(jnp.float32))
    return (denoised, grad_first, grad_second)
```

```python
import jax
import jax.numpy as jnp
from jax import lax
from jax.experimental import pallas as pl
from jax.sharding import PartitionSpec as P

HEADS = 16
HEAD_DIM = 64
BACK_CHUNKS = 4
FIRST_CHUNKS = 2


def normalize(part):
    count, columns = part.shape
    shaped = part.reshape(count, columns // HEAD_DIM, HEAD_DIM)
    meansq = jnp.mean(shaped * shaped, axis=-1, keepdims=True)
    return (shaped * lax.rsqrt(meansq + 1e-06)).astype(jnp.bfloat16).reshape(count, columns)


def attend(queries, key_piece, value_piece):
    query_count, columns = queries.shape
    key_count = key_piece.shape[0]
    heads = columns // HEAD_DIM
    query_heads = queries.reshape(query_count, heads, HEAD_DIM)
    key_heads = key_piece.reshape(key_count, heads, HEAD_DIM)
    value_heads = value_piece.reshape(key_count, heads, HEAD_DIM)
    scores = jnp.einsum(
        "qhd,khd->hqk", query_heads, key_heads, preferred_element_type=jnp.float32
    ) * HEAD_DIM ** (-0.5)
    expw = jnp.exp(scores).astype(jnp.bfloat16)
    denom = jnp.sum(expw, axis=2, dtype=jnp.float32)
    numer = jnp.einsum("hqk,khd->qhd", expw, value_heads, preferred_element_type=jnp.float32)
    return (numer / denom.T[:, :, None]).astype(jnp.bfloat16).reshape(query_count, columns)


def scattered_projection(masked_in, weight, groups, kinds):
    rows = masked_in.shape[0]
    part = jnp.dot(masked_in, weight, preferred_element_type=jnp.float32).astype(jnp.bfloat16)
    if HEADS % groups:
        return lax.psum(part, "gene").astype(jnp.float32).reshape(rows, kinds, -1)
    if kinds == 1:
        share = lax.psum_scatter(part, "gene", scatter_dimension=1, tiled=True)
        return share.astype(jnp.float32).reshape(rows, 1, -1)
    apart = part.reshape(rows, kinds, groups, -1).transpose(2, 1, 0, 3)
    share = lax.psum_scatter(apart, "gene", scatter_dimension=0, tiled=False)
    return share.transpose(1, 0, 2).astype(jnp.float32)


def cost(flops, moved):
    return pl.CostEstimate(flops=flops, bytes_accessed=moved, transcendentals=0)


def back_body(cot_ref, weight_ref, *out_refs):
    groups, _, pair, step, _ = out_refs[0].shape
    rows = lax.dot_general(
        weight_ref[0], cot_ref[...], (((1,), (1,)), ((), ())), preferred_element_type=jnp.float32
    )
    for index, out_ref in enumerate(out_refs):
        for g in range(groups):
            for r in range(pair):
                start = ((r * groups + g) * len(out_refs) + index) * step
                out_ref[g, 0, r] = rows[start : start + step].astype(out_ref.dtype)


def back_factor(cotangent, w_second, groups, pair, chunks):
    cells = cotangent.shape[0]
    local_blocks, block_size, _ = w_second.shape
    step = local_blocks // chunks
    return pl.pallas_call(
        back_body,
        grid=(local_blocks,),
        in_specs=[
            pl.BlockSpec((cells, block_size), lambda j: (0, j)),
            pl.BlockSpec((1, block_size, block_size), lambda j: (j, 0, 0)),
        ],
        out_specs=[
            pl.BlockSpec((groups, 1, pair, step, cells), lambda j: (0, j, 0, 0, 0))
        ]
        * chunks,
        out_shape=[
            jax.ShapeDtypeStruct((groups, local_blocks, pair, step, cells), jnp.bfloat16)
        ]
        * chunks,
        cost_estimate=cost(
            2 * cells * local_blocks * block_size**2, 5 * cells * local_blocks * block_size
        ),
    )(cotangent, w_second)


def first_body(attended_ref, out_weight_ref, masked_ref, weight_ref, hidden_ref, *first_refs):
    groups, _, step, _ = first_refs[0].shape
    added = jnp.dot(attended_ref[...], out_weight_ref[...], preferred_element_type=jnp.float32)
    hidden = (masked_ref[...].astype(jnp.float32) + added).astype(hidden_ref.dtype)
    hidden_ref[...] = hidden
    rows = lax.dot_general(
        weight_ref[0], hidden, (((0,), (1,)), ((), ())), preferred_element_type=jnp.float32
    )
    for index, first_ref in enumerate(first_refs):
        for g in range(groups):
            start = (g * len(first_refs) + index) * step
            first_ref[g, 0] = rows[start : start + step].astype(first_ref.dtype)


def first_factor(attended, w_out, masked_in, w_first, groups, chunks):
    cells, width = attended.shape
    local_blocks, block_size, _ = w_first.shape
    step = block_size // groups // chunks
    columns = pl.BlockSpec((cells, block_size), lambda b: (0, b))
    return pl.pallas_call(
        first_body,
        grid=(local_blocks,),
        in_specs=[
            pl.BlockSpec((cells, width), lambda b: (0, 0)),
            pl.BlockSpec((width, block_size), lambda b: (0, b)),
            columns,
            pl.BlockSpec((1, block_size, block_size), lambda b: (b, 0, 0)),
        ],
        out_specs=[columns]
        + [pl.BlockSpec((groups, 1, step, cells), lambda b: (0, b, 0, 0))] * chunks,
        out_shape=[jax.ShapeDtypeStruct(masked_in.shape, jnp.bfloat16)]
        + [jax.ShapeDtypeStruct((groups, local_blocks, step, cells), jnp.bfloat16)] * chunks,
        cost_estimate=cost(
            2 * cells * local_blocks * block_size * (block_size + width),
            2 * local_blocks * block_size * (3 * cells + width + block_size),
        ),
    )(attended, w_out, masked_in, w_first)


def grad_body(got_ref, hidden_ref, grad_ref):
    rows = jnp.dot(got_ref[0], hidden_ref[...], preferred_element_type=jnp.float32)
    grad_ref[0] = rows.T.astype(grad_ref.dtype)


def first_gradient(got, hidden, at, step):
    _, block_size, cells = got.shape
    return pl.pallas_call(
        grad_body,
        grid=(step,),
        in_specs=[
            pl.BlockSpec((1, block_size, cells), lambda b: (at + b, 0, 0)),
            pl.BlockSpec((cells, block_size), lambda b: (0, at + b)),
        ],
        out_specs=pl.BlockSpec((1, block_size, block_size), lambda b: (b, 0, 0)),
        out_shape=jax.ShapeDtypeStruct((step, block_size, block_size), jnp.bfloat16),
        cost_estimate=cost(2 * step * cells * block_size**2, 5 * step * cells * block_size),
    )(got, hidden)


def second_body(permuted_ref, cot_ref, hidden_ref, weight_ref, *rest):
    out_ref, grad_ref = rest[-2:]
    permuted = permuted_ref[0]
    mixed = lax.dot_general(
        permuted, weight_ref[0], (((0,), (0,)), ((), ())), preferred_element_type=jnp.float32
    )
    out_ref[...] = (hidden_ref[...].astype(jnp.float32) + mixed).astype(out_ref.dtype)
    grad_ref[0] = jnp.dot(
        permuted, cot_ref[...], preferred_element_type=jnp.float32
    ).astype(grad_ref.dtype)


def second_factor(permuted, cotangent, hidden, w_second, at, denoised):
    step, block_size, cells = permuted.shape
    columns = pl.BlockSpec((cells, block_size), lambda j: (0, at + j))
    in_specs = [
        pl.BlockSpec((1, block_size, cells), lambda j: (j, 0, 0)),
        columns,
        columns,
        pl.BlockSpec((1, block_size, block_size), lambda j: (at + j, 0, 0)),
    ]
    operands = [permuted, cotangent, hidden, w_second]
    aliases = {}
    if denoised is not None:
        in_specs.append(pl.BlockSpec(memory_space=pl.ANY))
        operands.append(denoised)
        aliases = {4: 0}
    return pl.pallas_call(
        second_body,
        grid=(step,),
        in_specs=in_specs,
        out_specs=[columns, pl.BlockSpec((1, block_size, block_size), lambda j: (j, 0, 0))],
        out_shape=[
            jax.ShapeDtypeStruct(hidden.shape, jnp.bfloat16),
            jax.ShapeDtypeStruct((step, block_size, block_size), jnp.bfloat16),
        ],
        input_output_aliases=aliases,
        cost_estimate=cost(4 * step * cells * block_size**2, 10 * step * cells * block_size),
    )(*operands)


def on_device(expression, gene_mask, mask_value, w_qkv, w_out, w_first, w_second, cotangent):
    groups = lax.axis_size("gene")
    local_blocks, block_size, _ = w_first.shape
    cell_rows = expression.shape[0]
    width = w_qkv.shape[1] // 3
    pair = block_size // (local_blocks * groups)

    back_chunks = max(min(BACK_CHUNKS, local_blocks // 8), 1)
    back_step = local_blocks // back_chunks
    backs = back_factor(cotangent, w_second, groups, pair, back_chunks)
    backs, expression, gene_mask = lax.optimization_barrier((backs, expression, gene_mask))
    back_recv = [
        lax.all_to_all(back, "gene", split_axis=0, concat_axis=0, tiled=True) for back in backs
    ]

    masked_in = jnp.where(gene_mask == 1, mask_value[None, :], expression)
    masked_late, back_recv[0] = lax.optimization_barrier((masked_in, back_recv[0]))
    query_sum = scattered_projection(masked_late, w_qkv[:, :width], groups, 1)[:, 0]
    pair_sum = scattered_projection(masked_in, w_qkv[:, width:], groups, 2)
    columns = pair_sum.shape[2]
    pieces = jnp.concatenate(
        [normalize(pair_sum[:, 0]), pair_sum[:, 1].astype(jnp.bfloat16)], axis=1
    )
    gathered = lax.all_gather(pieces, "cell", axis=0, tiled=True)
    attended = attend(normalize(query_sum), gathered[:, :columns], gathered[:, columns:])
    if HEADS % groups == 0:
        attended = lax.all_gather(attended, "gene", axis=1, tiled=True)

    first_chunks = max(min(FIRST_CHUNKS, local_blocks * pair // 16), 1)
    first_step = local_blocks // first_chunks
    hidden, *firsts = first_factor(attended, w_out, masked_in, w_first, groups, first_chunks)
    firsts, back_recv = lax.optimization_barrier((firsts, back_recv))
    recv = [
        lax.all_to_all(first, "gene", split_axis=0, concat_axis=0, tiled=True) for first in firsts
    ]

    def share(grad):
        return lax.psum_scatter(
            grad.astype(jnp.bfloat16), "cell", scatter_dimension=1, tiled=True
        ).astype(jnp.float32)

    got = jnp.concatenate([back.transpose(3, 0, 1, 2, 4) for back in back_recv], axis=0)
    got = got.reshape(local_blocks, block_size, cell_rows)
    first_grads = [first_gradient(got, hidden, 0, local_blocks)]
    recv[0], first_grads = lax.optimization_barrier((recv[0], first_grads))
    first_shares = [share(grad) for grad in first_grads]

    denoised, second_shares = None, []
    for index, at in enumerate(range(0, local_blocks, first_step)):
        permuted = (
            recv[index]
            .reshape(groups, local_blocks, first_step, pair, cell_rows)
            .transpose(2, 3, 0, 1, 4)
            .reshape(first_step, block_size, cell_rows)
        )
        denoised, grad_second = second_factor(
            permuted, cotangent, hidden, w_second, at, denoised
        )
        second_shares.append(share(grad_second))
        if index == first_chunks - 3:
            denoised, second_shares = lax.optimization_barrier((denoised, second_shares))
        if index == first_chunks - 2:
            denoised, first_shares = lax.optimization_barrier((denoised, first_shares))
    return (
        denoised,
        jnp.concatenate(first_shares, axis=0),
        jnp.concatenate(second_shares, axis=0),
    )


def solution(mesh):
    placed = (
        P(("grp", "cell"), "gene"),
        P(("grp", "cell"), "gene"),
        P("gene"),
        P("gene", None),
        P(None, "gene"),
        P("gene", None, None),
        P("gene", None, None),
        P(("grp", "cell"), "gene"),
    )
    return jax.shard_map(
        on_device,
        mesh=mesh,
        in_specs=placed,
        out_specs=(
            P(("grp", "cell"), "gene"),
            P(("grp", "gene"), "cell", None),
            P(("grp", "gene"), "cell", None),
        ),
        check_vma=False,
    )
```
